256 devices in a mesh: row: 8 (over z_lo, y), col: 32 (over x, z_hi, core).
Axes of the slice: x: 4, y: 4, z: 8 (z_hi: 4, z_lo: 2; z = z_hi * 2 + z_lo), core: 2. Of those that a mesh axis runs over, the one named last changes fastest.
Arguments:
- ancestor_inv: float32 [16384, 16384], P('row', 'col'), may hold values from -0.09375 to 0.09375
- factor_rows: float32 [16384, 768], P(('row', 'col')), may hold values from -1.2 to 1.2
- diagonal_inv: float32 [3, 256, 256], replicated, may hold values from -6 to 6
- fill_list: int32 [3, 64], replicated, may hold values 0 or 1
Outputs:
- column_block: float32 [16384, 768], P(('row', 'col'))
- diagonal_block: float32 [3, 256, 256], replicated
The draws below stay inside these ranges and needn't reach their ends.
All inputs are finite; a program needn't handle non-finite values.
Results may differ from the reference program's by a relative error of at most 0.000071.
Values sent between devices are 32-bit elements; how exact they have to be, the bound alone decides.
A program may use at most 64 MiB of HBM per device.

```python
import jax
import jax.numpy as jnp
from jax import lax

R = 16384
W = 256
SIBS = 3
TILE = 256
NB = 64


def touch_ends(result, stream_key, low, top_value):
    shape = result.shape
    index_at = [jax.random.randint(jax.random.fold_in(stream_key, axis), (), 0, shape[axis]) for axis in range(len(shape))]
    result = result.at[tuple(index_at)].set(low)
    longest = shape.index(max(shape))
    index_at[longest] = (index_at[longest] + 1) % shape[longest]
    return result.at[tuple(index_at)].set(top_value)


def raised(array, rng, source, target, blocks, factor):
    owner, partner = [(jnp.arange(array.shape[dim]) // (array.shape[dim] // blocks)).reshape([-1 if axis == dim else 1 for axis in range(array.ndim)]) for dim in (source, target)]
    chosen = jax.random.permutation(rng, blocks)[partner]
    strong = (owner == chosen) | (owner == (partner + blocks // 2) % blocks)
    return jnp.where(strong, factor * array, array)


def block_scale(own_key, dims, cuts, least, high):
    def one(position, blocks):
        steps = jax.random.uniform(jax.random.fold_in(jax.random.fold_in(own_key, 6), position), (blocks,), jnp.float32, least / len(cuts), high / len(cuts))
        return jnp.repeat(jnp.exp(steps), dims[position] // blocks).reshape((-1,) + (1,) * (len(dims) - position - 1))

    gain = one(*cuts[0])
    for cut in cuts[1:]:
        gain = gain * one(*cut)
    return gain


def normal_values(stream_key, shape, scale, bound, pieces=(), kind=jnp.bfloat16):
    array = jax.random.normal(stream_key, shape, jnp.float32) * scale
    if len(pieces) > 0:
        array = block_scale(stream_key, shape, pieces, -0.22, 0.18) * array
    return jnp.clip(array, min=-bound, max=bound).astype(kind)


def bell_draw_with(rng, dims, width, most, cuts, heavy, held_as=jnp.bfloat16):
    drawn = width * jax.random.normal(rng, dims, jnp.float32)
    if cuts:
        drawn = drawn * block_scale(rng, dims, cuts, -0.22, 0.18)
    return jnp.clip(raised(drawn, jax.random.fold_in(rng, 3), *heavy), -most, most).astype(held_as)


def setup_inputs(seed: int = 0) -> dict:
    seeds = jax.random.split(jax.random.key(seed), 5)
    ancestor_inv = bell_draw_with(seeds[0], (R, R), R ** -0.5, 0.09375, ((0, 8), (1, 32)), (1, 0, 32, 2.75), jnp.float32)
    factor_rows = normal_values(seeds[1], (R, SIBS * W), 0.2, 1.2, ((0, 256),), jnp.float32)
    diagonal_inv = normal_values(seeds[2], (SIBS, W, W), 1.0, 6.0, (), jnp.float32)
    fill_list = touch_ends((jax.random.randint(seeds[3], (SIBS, NB), 0, 2) < 1).astype(jnp.int32), jax.random.fold_in(seeds[3], 1), 0, 1)
    return {"ancestor_inv": ancestor_inv, "factor_rows": factor_rows, "diagonal_inv": diagonal_inv, "fill_list": fill_list}


def reference(ancestor_inv, factor_rows, diagonal_inv, fill_list):
    tile_index = jnp.arange(R, dtype=jnp.int32) // TILE
    one_hot = (tile_index[:, None] == jnp.arange(NB, dtype=jnp.int32)[None, :]).astype(jnp.float32)
    row_mask = jnp.dot(one_hot, fill_list.T.astype(jnp.float32), precision=lax.Precision.HIGHEST)
    wide_mask = jnp.repeat(row_mask, W, axis=1)
    masked = factor_rows * wide_mask
    product = jnp.dot(ancestor_inv, masked, precision=lax.Precision.HIGHEST)
    column_block = -product * wide_mask
    left_side = masked.reshape(R, SIBS, W)
    right_side = column_block.reshape(R, SIBS, W)
    update = jnp.einsum("rkw,rkv->kwv", left_side, right_side, precision=lax.Precision.HIGHEST)
    return column_block, diagonal_inv - update
```

```python
import functools

import jax
import jax.numpy as jnp
from jax import lax
from jax.experimental import pallas as pl
from jax.experimental.pallas import tpu as pltpu
from jax.sharding import PartitionSpec as P

W = 256
SIBS = 3
HALF = 128
F32 = jnp.float32
BF16 = jnp.bfloat16


def split(v):
    high = v.astype(BF16)
    return high, (v - high.astype(F32)).astype(BF16)


def three_pass(a_high, a_low, b_high, b_low):
    dot = functools.partial(jnp.dot, preferred_element_type=F32)
    return dot(a_high, b_high) + (dot(a_high, b_low) + dot(a_low, b_high))


def kernel(
    fill, fac, a_in, d_in, cb, dg,
    a_own, a_rec, a_high, a_low, m_own, m_rec, m_high, m_low, f_own, f_rec, t_high, t_low, d_slab,
    prod, xa, xr, zb, c_own, c_rec, u, rs, zs, g,
    local_sem, perm_s, perm_r, one_s, one_r, ag_s, ag_r, x_s, x_r, z_s, z_r, c_s, c_r,
    p_s, p_r, e_s, e_r, q_s, q_r, h_s, h_r,
):
    r = lax.axis_index("row")
    c = lax.axis_index("col")
    zl, y = lax.div(r, 4), lax.rem(r, 4)
    x, zh, core = lax.div(c, 8), lax.rem(lax.div(c, 2), 4), lax.rem(c, 2)
    z = zh * 2 + zl
    other = 1 - core
    slab = x * 4 + y

    def wrap(v, n):
        return lax.rem(v + n, n)

    def at(x_, y_, z_, core_):
        return (lax.rem(z_, 2) * 4 + y_, x_ * 8 + lax.div(z_, 2) * 2 + core_)

    def swap(v):
        return v + 1 - 2 * lax.rem(v, 2)

    partner = at(x, y, z, other)
    y_up, y_down = wrap(y + 1, 4), wrap(y - 1, 4)
    y_far = wrap(y + 2, 4)
    up, down = at(x, y_up, z, core), at(x, y_down, z, core)
    right, left = at(wrap(x + 1, 4), y, z, core), at(wrap(x - 1, 4), y, z, core)
    twin = at(x, y, zh * 2 + 1 - zl, core)
    piece = lax.rem(c, 8)
    target = (swap(piece), r * 4 + x)
    source_index = c * 8 + swap(r)
    source = (lax.div(source_index, 32), lax.rem(source_index, 32))

    def plane(d):
        return wrap(x + lax.div(d, 4), 4), wrap(y + lax.rem(d, 4), 4)

    barrier = pltpu.get_barrier_semaphore()

    def hello(device):
        pl.semaphore_signal(barrier, inc=1, device_id=device, device_id_type=pl.DeviceIdType.MESH)

    @pl.loop(1, 16)
    def _(d):
        px, py = plane(d)
        hello(at(px, py, z, core))

    @pl.loop(1, 8)
    def _(d):
        hello(at(x, y, wrap(z + d, 8), core))

    hello(partner)
    hello(target)
    hello(source)

    own_rows = pltpu.make_async_copy(a_in.at[:, core], a_own, local_sem.at[0])
    own_rows.start()
    own_factor = pltpu.make_async_copy(fac, f_own, local_sem.at[1])
    own_factor.start()
    own_diag = pltpu.make_async_copy(
        d_in.at[:, pl.ds(pl.multiple_of(slab * 16, 16), 16), pl.ds(pl.multiple_of(core * HALF, HALF), HALF)],
        d_slab,
        local_sem.at[2],
    )
    own_diag.start()
    pl.semaphore_wait(barrier, 25)

    sent = []

    def copy(src, dst, ssem, rsem, device):
        return pltpu.make_async_remote_copy(
            src_ref=src, dst_ref=dst, send_sem=ssem, recv_sem=rsem,
            device_id=device, device_id_type=pl.DeviceIdType.MESH,
        )

    def send(src, dst, ssem, rsem, device):
        out = copy(src, dst, ssem, rsem, device)
        out.start()
        sent.append(out)

    def arrived(dst, ssem, rsem):
        copy(dst, dst, ssem, rsem, partner).wait_recv()

    yme, ydn, yup, yfar = swap(y), swap(y_down), swap(y_up), swap(y_far)
    for k in range(SIBS):
        landing = m_own.at[k, lax.rem(piece, 4), lax.div(piece, 4)]
        send(fac.at[:, pl.ds(k * W, W)], landing, perm_s.at[k], perm_r.at[k], target)
    send(a_in.at[:, other], a_rec, one_s.at[0], one_r.at[0], partner)
    send(fac, f_rec, one_s.at[1], one_r.at[1], partner)

    def split_rows(src, column):
        @pl.loop(0, 16)
        def _(i):
            rows = pl.ds(pl.multiple_of(i * 64, 64), 64)
            high, low = split(src[i])
            a_high[rows, column : column + 512] = high
            a_low[rows, column : column + 512] = low

    def ag(k, n, src, dst, device):
        send(src, dst, ag_s.at[k, n], ag_r.at[k, n], device)

    def ag_in(k, n, dst):
        arrived(dst, ag_s.at[k, n], ag_r.at[k, n])

    def gather_a(k):
        own = m_own.at[k, yme, zl]
        arrived(own, perm_s.at[k], perm_r.at[k])
        ag(k, 0, own, own, twin)
        ag(k, 1, own, own, up)
        ag(k, 2, own, own, down)
        ag(k, 3, own, m_rec.at[k, yme, zl], partner)

    def gather_b(k):
        own = m_own.at[k, yme, 1 - zl]
        ag_in(k, 0, own)
        ag(k, 4, own, own, up)
        ag(k, 5, own, own, down)
        ag(k, 6, own, m_rec.at[k, yme, 1 - zl], partner)

    def gather_c(k):
        low = m_own.at[k, ydn, zl]
        ag_in(k, 1, low)
        ag(k, 7, low, low, up)
        high = m_own.at[k, yup, 1 - zl]
        ag_in(k, 5, high)
        ag(k, 8, high, high, down)

    def gather_d(k):
        ag_in(k, 4, m_own.at[k, ydn, 1 - zl])
        ag(k, 9, m_own.at[k, ydn], m_rec.at[k, ydn], partner)
        ag_in(k, 2, m_own.at[k, yup, zl])
        ag(k, 10, m_own.at[k, yup], m_rec.at[k, yup], partner)
        ag_in(k, 7, m_own.at[k, yfar, zl])
        ag_in(k, 8, m_own.at[k, yfar, 1 - zl])
        ag(k, 11, m_own.at[k, yfar], m_rec.at[k, yfar], partner)

    def split_pieces(k, src, column, first):
        for half in range(2):
            mask = fill[k, 2 * column + half].astype(F32)
            for n in range(4):
                row = first + (half * 4 + n) * 64
                high, low = split(src[k, n, half] * mask)
                m_high[k, row : row + 64] = high
                m_low[k, row : row + 64] = low

    def gather_e(k):
        split_pieces(k, m_own, c, 0)
        ag_in(k, 3, m_rec.at[k, yme, zl])
        ag_in(k, 6, m_rec.at[k, yme, 1 - zl])
        ag_in(k, 9, m_rec.at[k, ydn])
        ag_in(k, 10, m_rec.at[k, yup])
        ag_in(k, 11, m_rec.at[k, yfar])
        split_pieces(k, m_rec, swap(c), 512)

    own_tile = r * 8 + lax.div(c, 4)

    def own_masks():
        own_factor.wait()
        arrived(f_rec, one_s.at[1], one_r.at[1])
        for k in range(SIBS):
            mask = fill[k, own_tile].astype(F32)
            for n, src in enumerate((f_own, f_rec)):
                turned = (src[:, k * W : (k + 1) * W] * mask).T
                high, low = split(turned)
                t_high[k, :, n * 64 : (n + 1) * 64] = high
                t_low[k, :, n * 64 : (n + 1) * 64] = low

    def multiply(k, away):
        rows = pl.ds(pl.multiple_of(wrap(x + away, 4) * 256, 256), 256)
        result = three_pass(a_high[rows, :], a_low[rows, :], m_high[k], m_low[k])
        prod[k, away] = result.reshape(4, 64, W)

    def xs(k, n, src, device):
        send(src, xa.at[k, n], x_s.at[k, n], x_r.at[k, n], device)

    def x_in(k, n):
        arrived(xa.at[k, n], x_s.at[k, n], x_r.at[k, n])

    def x_one(k):
        multiply(k, 2)
        xs(k, 0, prod.at[k, 2, pl.ds(0, 2)], right)
        xs(k, 1, prod.at[k, 2, pl.ds(2, 2)], left)

    def x_two(k):
        multiply(k, 1)
        xs(k, 2, prod.at[k, 1, pl.ds(2, 2)], right)
        multiply(k, 3)
        xs(k, 3, prod.at[k, 3, pl.ds(0, 2)], left)

    def x_three(k):
        x_in(k, 0)
        prod[k, 1, 0:2] = prod[k, 1, 0:2] + xa[k, 0]
        xs(k, 4, prod.at[k, 1, pl.ds(0, 2)], right)
        x_in(k, 1)
        prod[k, 3, 2:4] = prod[k, 3, 2:4] + xa[k, 1]
        xs(k, 5, prod.at[k, 3, pl.ds(2, 2)], left)

    def x_sum(k):
        x_in(k, 3)
        x_in(k, 4)
        xr[k, 0:2] = prod[k, 0, 0:2] + xa[k, 4] + xa[k, 3]
        x_in(k, 2)
        x_in(k, 5)
        xr[k, 2:4] = prod[k, 0, 2:4] + xa[k, 2] + xa[k, 5]
        for d in (2, 1, 3):
            there = wrap(zh + d, 4)
            send(xr.at[k, there], zb.at[k, d - 1], z_s.at[k, d - 1], z_r.at[k, d - 1], at(x, y, there * 2 + zl, core))

    def z_sum(k):
        for d in range(3):
            arrived(zb.at[k, d], z_s.at[k, d], z_r.at[k, d])
        mask = fill[k, own_tile].astype(F32)
        block = -(xr[k, zh] + zb[k, 0] + zb[k, 1] + zb[k, 2]) * mask
        cb[:, k * W : (k + 1) * W] = block
        c_own[k, 0] = block[:, :HALF]
        c_own[k, 1] = block[:, HALF:]
        send(c_own.at[k, other], c_rec.at[k], c_s.at[k], c_r.at[k], partner)

    def local_term(k):
        t_h, t_l = t_high[k], t_low[k]
        arrived(c_rec.at[k], c_s.at[k], c_r.at[k])
        high, low = split(jnp.concatenate([c_own[k, core], c_rec[k]], axis=0))
        u[k] = three_pass(t_h, t_l, high, low).reshape(16, 16, HALF)

        @pl.loop(1, 16)
        def _(d):
            px, py = plane(d)
            copy(u.at[k, px * 4 + py], rs.at[k, d], p_s.at[k, d], p_r.at[k, d], at(px, py, z, core)).start()

    def plane_sum(k):
        total = u[k, slab]
        for d in range(1, 16):
            arrived(rs.at[k, d], p_s.at[k, d], p_r.at[k, d])
            total = total + rs[k, d]
        zs[k, z] = total

        @pl.loop(1, 8)
        def _(d):
            to = at(x, y, wrap(z + d, 8), core)
            copy(zs.at[k, z], zs.at[k, z], e_s.at[k, d], e_r.at[k, d], to).start()

    def line_sum(k):
        @pl.loop(1, 8)
        def _(d):
            arrived(zs.at[k, wrap(z - d, 8)], e_s.at[k, d], e_r.at[k, d])

        total = zs[k, 0]
        for n in range(1, 8):
            total = total + zs[k, n]
        g[k, core, slab] = d_slab[k] - total

        @pl.loop(1, 16)
        def _(d):
            px, py = plane(d)
            mine = g.at[k, core, slab]
            copy(mine, mine, q_s.at[k, d], q_r.at[k, d], at(px, py, z, core)).start()

    def spread(k):
        @pl.loop(1, 16)
        def _(d):
            px, py = wrap(x - lax.div(d, 4), 4), wrap(y - lax.rem(d, 4), 4)
            arrived(g.at[k, core, px * 4 + py], q_s.at[k, d], q_r.at[k, d])

        send(g.at[k, core], g.at[k, core], h_s.at[k], h_r.at[k], partner)

    def finish(k):
        arrived(g.at[k, other], h_s.at[k], h_r.at[k])
        dg[k, :, 0:HALF] = g[k, 0].reshape(W, HALF)
        dg[k, :, HALF:W] = g[k, 1].reshape(W, HALF)

    own_rows.wait()
    split_rows(a_own, 0)
    gather_a(0)
    gather_a(1)
    gather_b(0)
    gather_a(2)
    gather_c(0)
    gather_b(1)
    arrived(a_rec, one_s.at[0], one_r.at[0])
    split_rows(a_rec, 512)
    gather_d(0)
    gather_c(1)
    gather_b(2)
    gather_e(0)
    x_one(0)
    gather_d(1)
    x_two(0)
    gather_c(2)
    gather_e(1)
    x_one(1)
    gather_d(2)
    x_three(0)
    x_two(1)
    gather_e(2)
    x_one(2)
    own_diag.wait()
    own_masks()
    multiply(0, 0)
    x_three(1)
    x_two(2)
    multiply(1, 0)
    x_sum(0)
    multiply(2, 0)
    x_three(2)
    z_sum(0)
    local_term(0)
    x_sum(1)
    plane_sum(0)
    x_sum(2)
    z_sum(1)
    local_term(1)
    line_sum(0)
    z_sum(2)
    local_term(2)
    plane_sum(1)
    spread(0)
    line_sum(1)
    plane_sum(2)
    finish(0)
    spread(1)
    line_sum(2)
    finish(1)
    spread(2)
    finish(2)

    for out in sent:
        out.wait_send()
    for k in range(SIBS):

        @pl.loop(1, 16)
        def _(d):
            copy(u.at[k, 0], rs.at[k, d], p_s.at[k, d], p_r.at[k, d], partner).wait_send()
            copy(g.at[k, core, slab], g.at[k, core, slab], q_s.at[k, d], q_r.at[k, d], partner).wait_send()

        @pl.loop(1, 8)
        def _(d):
            copy(zs.at[k, z], zs.at[k, z], e_s.at[k, d], e_r.at[k, d], partner).wait_send()


def local(ancestor_inv, factor_rows, diagonal_inv, fill_list):
    vmem, dma = pltpu.VMEM, pltpu.SemaphoreType.DMA
    hbm = pl.BlockSpec(memory_space=pl.ANY)
    pairs = [(SIBS,), (2,), (SIBS, 12), (SIBS, 6), (SIBS, 3), (SIBS,), (SIBS, 16), (SIBS, 8), (SIBS, 16), (SIBS,)]
    return pl.pallas_call(
        kernel,
        out_shape=(
            jax.ShapeDtypeStruct(factor_rows.shape, F32),
            jax.ShapeDtypeStruct(diagonal_inv.shape, F32),
        ),
        in_specs=[pl.BlockSpec(memory_space=pltpu.SMEM), hbm, hbm, hbm],
        out_specs=[pl.BlockSpec(memory_space=pltpu.VMEM)] * 2,
        scratch_shapes=[
            vmem((16, 64, 512), F32),
            vmem((16, 64, 512), F32),
            vmem((1024, 1024), BF16),
            vmem((1024, 1024), BF16),
            vmem((SIBS, 4, 2, 64, W), F32),
            vmem((SIBS, 4, 2, 64, W), F32),
            vmem((SIBS, 1024, W), BF16),
            vmem((SIBS, 1024, W), BF16),
            vmem((64, SIBS * W), F32),
            vmem((64, SIBS * W), F32),
            vmem((SIBS, W, 128), BF16),
            vmem((SIBS, W, 128), BF16),
            vmem((SIBS, 16, HALF), F32),
            vmem((SIBS, 4, 4, 64, W), F32),
            vmem((SIBS, 6, 2, 64, W), F32),
            vmem((SIBS, 4, 64, W), F32),
            vmem((SIBS, 3, 64, W), F32),
            vmem((SIBS, 2, 64, HALF), F32),
            vmem((SIBS, 64, HALF), F32),
            vmem((SIBS, 16, 16, HALF), F32),
            vmem((SIBS, 16, 16, HALF), F32),
            vmem((SIBS, 8, 16, HALF), F32),
            vmem((SIBS, 2, 16, 16, HALF), F32),
            dma((3,)),
        ]
        + [dma(shape) for shape in pairs for _ in range(2)],
        compiler_params=pltpu.CompilerParams(
            collective_id=0, has_side_effects=True, vmem_limit_bytes=56 * 1024 * 1024
        ),
    )(fill_list, factor_rows, ancestor_inv.reshape(16, 2, 64, 512), diagonal_inv)


def solution(mesh):
    placed = (P("row", "col"), P(("row", "col"), None), P(), P())
    return jax.shard_map(
        local, mesh=mesh, in_specs=placed, out_specs=(P(("row", "col"), None), P()), check_vma=False
    )
```

```python
import functools

import jax
import jax.numpy as jnp
from jax import lax
from jax.experimental import pallas as pl
from jax.experimental.pallas import tpu as pltpu
from jax.sharding import PartitionSpec as P

W = 256
SIBS = 3
HALF = 128
F32 = jnp.float32
BF16 = jnp.bfloat16


def split(v):
    high = v.astype(BF16)
    return high, (v - high.astype(F32)).astype(BF16)


def three_pass(a_high, a_low, b_high, b_low):
    dot = functools.partial(jnp.dot, preferred_element_type=F32)
    return dot(a_high, b_high) + (dot(a_high, b_low) + dot(a_low, b_high))


def kernel(
    fill, fac, a_in, d_in, cb, dg,
    a_own, a_rec, a_high, a_low, m_own, m_rec, m_high, m_low, f_own, f_rec, t_high, t_low, d_slab,
    turn, prod, xa, xr, zb, c_own, c_rec, u, rs, zs, g,
    local_sem, turn_s, turn_r, perm_s, perm_r, one_s, one_r, ag_s, ag_r, x_s, x_r, z_s, z_r, c_s, c_r,
    p_s, p_r, e_s, e_r, q_s, q_r, h_s, h_r,
):
    r = lax.axis_index("row")
    c = lax.axis_index("col")
    zl, y = lax.div(r, 4), lax.rem(r, 4)
    x, zh, core = lax.div(c, 8), lax.rem(lax.div(c, 2), 4), lax.rem(c, 2)
    z = zh * 2 + zl
    other = 1 - core
    slab = x * 4 + y

    def wrap(v, n):
        return lax.rem(v + n, n)

    def at(x_, y_, z_, core_):
        return (lax.rem(z_, 2) * 4 + y_, x_ * 8 + lax.div(z_, 2) * 2 + core_)

    def swap(v):
        return v + 1 - 2 * lax.rem(v, 2)

    partner = at(x, y, z, other)
    y_up, y_down = wrap(y + 1, 4), wrap(y - 1, 4)
    y_far = wrap(y + 2, 4)
    up, down = at(x, y_up, z, core), at(x, y_down, z, core)
    right, left = at(wrap(x + 1, 4), y, z, core), at(wrap(x - 1, 4), y, z, core)
    twin = at(x, y, zh * 2 + 1 - zl, core)
    part = lax.div(zh, 2) * 2 + core

    def target(y_from):
        z_to = (2 * lax.rem(y_from, 2) + lax.div(x, 2)) * 2 + 1 - lax.rem(zh, 2)
        return at(2 * zl + lax.div(y_from, 2), y, z_to, lax.rem(x, 2))

    def source(n):
        z_from = ((n // 2) * 2 + 1 - zl) * 2 + lax.div(x, 2)
        return at(2 * lax.rem(zh, 2) + core, y, z_from, n % 2)

    def plane(d):
        return wrap(x + lax.div(d, 4), 4), wrap(y + lax.rem(d, 4), 4)

    barrier = pltpu.get_barrier_semaphore()

    def hello(device):
        pl.semaphore_signal(barrier, inc=1, device_id=device, device_id_type=pl.DeviceIdType.MESH)

    @pl.loop(1, 16)
    def _(d):
        px, py = plane(d)
        hello(at(px, py, z, core))

    @pl.loop(1, 8)
    def _(d):
        hello(at(x, y, wrap(z + d, 8), core))

    hello(partner)
    for n in range(4):
        hello(target(n))
        hello(source(n))

    own_rows = pltpu.make_async_copy(a_in.at[:, core], a_own, local_sem.at[0])
    own_rows.start()
    own_factor = pltpu.make_async_copy(fac, f_own, local_sem.at[1])
    own_factor.start()
    own_diag = pltpu.make_async_copy(
        d_in.at[:, pl.ds(pl.multiple_of(slab * 16, 16), 16), pl.ds(pl.multiple_of(core * HALF, HALF), HALF)],
        d_slab,
        local_sem.at[2],
    )
    own_diag.start()

    def split_rows(src, column):
        @pl.loop(0, 16)
        def _(i):
            rows = pl.ds(pl.multiple_of(i * 64, 64), 64)
            high, low = split(src[i])
            a_high[rows, column : column + 512] = high
            a_low[rows, column : column + 512] = low

    own_rows.wait()
    split_rows(a_own, 0)
    pl.semaphore_wait(barrier, 31)

    sent = []

    def copy(src, dst, ssem, rsem, device):
        return pltpu.make_async_remote_copy(
            src_ref=src, dst_ref=dst, send_sem=ssem, recv_sem=rsem,
            device_id=device, device_id_type=pl.DeviceIdType.MESH,
        )

    def send(src, dst, ssem, rsem, device):
        out = copy(src, dst, ssem, rsem, device)
        out.start()
        sent.append(out)

    def arrived(dst, ssem, rsem):
        copy(dst, dst, ssem, rsem, partner).wait_recv()

    yme, ydn, yup, yfar = y, y_down, y_up, y_far

    def quarter(k, n):
        return fac.at[pl.ds(pl.multiple_of(n * 16, 16), 16), pl.ds(k * W, W)]

    def forward(k, n, y_from, src):
        landing = m_own.at[k, y, 1 - lax.rem(zh, 2), pl.ds(pl.multiple_of(part * 16, 16), 16)]
        send(src, landing, perm_s.at[k, n], perm_r.at[k, part], target(y_from))

    for k in range(SIBS):
        for d in (2, 1, 3):
            y_to = wrap(y + d, 4)
            send(quarter(k, y_to), turn.at[k, y], turn_s.at[k, d - 1], turn_r.at[k, d - 1], at(x, y_to, z, core))
        forward(k, 0, y, quarter(k, y))
    send(a_in.at[:, other], a_rec, one_s.at[0], one_r.at[0], partner)
    send(fac, f_rec, one_s.at[1], one_r.at[1], partner)

    def split_received(_):
        arrived(a_rec, one_s.at[0], one_r.at[0])
        split_rows(a_rec, 512)

    def ag(k, n, src, dst, device):
        send(src, dst, ag_s.at[k, n], ag_r.at[k, n], device)

    def ag_in(k, n, dst):
        arrived(dst, ag_s.at[k, n], ag_r.at[k, n])

    def turned(k):
        for d in (1, 3, 2):
            y_from = wrap(y - d, 4)
            arrived(turn.at[k, y_from], turn_s.at[k, d - 1], turn_r.at[k, d - 1])
            forward(k, d, y_from, turn.at[k, y_from])

    def gather_a(k):
        own = m_own.at[k, yme, zl]
        for n in range(4):
            arrived(m_own.at[k, yme, zl, pl.ds(n * 16, 16)], perm_s.at[k, n], perm_r.at[k, n])
        ag(k, 0, own, own, twin)
        ag(k, 1, own, own, up)
        ag(k, 2, own, own, down)
        ag(k, 3, own, m_rec.at[k, yme, zl], partner)

    def gather_b(k):
        own = m_own.at[k, yme, 1 - zl]
        ag_in(k, 0, own)
        ag(k, 4, own, own, up)
        ag(k, 5, own, own, down)
        ag(k, 6, own, m_rec.at[k, yme, 1 - zl], partner)

    def gather_c(k):
        low = m_own.at[k, ydn, zl]
        ag_in(k, 1, low)
        ag(k, 7, low, low, up)
        high = m_own.at[k, yup, 1 - zl]
        ag_in(k, 5, high)
        ag(k, 8, high, high, down)

    def gather_d(k):
        ag_in(k, 4, m_own.at[k, ydn, 1 - zl])
        ag(k, 9, m_own.at[k, ydn], m_rec.at[k, ydn], partner)
        ag_in(k, 2, m_own.at[k, yup, zl])
        ag(k, 10, m_own.at[k, yup], m_rec.at[k, yup], partner)
        ag_in(k, 7, m_own.at[k, yfar, zl])
        ag_in(k, 8, m_own.at[k, yfar, 1 - zl])
        ag(k, 11, m_own.at[k, yfar], m_rec.at[k, yfar], partner)

    def split_pieces(k, src, column, first):
        for n in range(4):
            mask = fill[k, 2 * column + n // 2].astype(F32)
            for half in range(2):
                piece = (n // 2) * 4 + (1 - half) * 2 + n % 2
                for m in range(4):
                    row = first + piece * 64 + m * 16
                    high, low = split(src[k, m, half, n * 16 : n * 16 + 16] * mask)
                    m_high[k, row : row + 16] = high
                    m_low[k, row : row + 16] = low

    def gather_e(k):
        split_pieces(k, m_own, c, 0)
        ag_in(k, 3, m_rec.at[k, yme, zl])
        ag_in(k, 6, m_rec.at[k, yme, 1 - zl])
        ag_in(k, 9, m_rec.at[k, ydn])
        ag_in(k, 10, m_rec.at[k, yup])
        ag_in(k, 11, m_rec.at[k, yfar])
        split_pieces(k, m_rec, swap(c), 512)

    own_tile = r * 8 + lax.div(c, 4)

    def own_masks(_):
        own_diag.wait()
        own_factor.wait()
        arrived(f_rec, one_s.at[1], one_r.at[1])
        for k in range(SIBS):
            mask = fill[k, own_tile].astype(F32)
            for n, src in enumerate((f_own, f_rec)):
                turned = (src[:, k * W : (k + 1) * W] * mask).T
                high, low = split(turned)
                t_high[k, :, n * 64 : (n + 1) * 64] = high
                t_low[k, :, n * 64 : (n + 1) * 64] = low

    def multiply(k, away):
        rows = pl.ds(pl.multiple_of(wrap(x + away, 4) * 256, 256), 256)
        result = three_pass(a_high[rows, :], a_low[rows, :], m_high[k], m_low[k])
        prod[k, away] = result.reshape(4, 64, W)

    def x_own(k):
        multiply(k, 0)

    def xs(k, n, src, device):
        send(src, xa.at[k, n], x_s.at[k, n], x_r.at[k, n], device)

    def x_in(k, n):
        arrived(xa.at[k, n], x_s.at[k, n], x_r.at[k, n])

    def x_one(k):
        multiply(k, 2)
        xs(k, 0, prod.at[k, 2, pl.ds(0, 2)], right)
        xs(k, 1, prod.at[k, 2, pl.ds(2, 2)], left)

    def x_two(k):
        multiply(k, 1)
        xs(k, 2, prod.at[k, 1, pl.ds(2, 2)], right)
        multiply(k, 3)
        xs(k, 3, prod.at[k, 3, pl.ds(0, 2)], left)

    def x_three(k):
        x_in(k, 0)
        prod[k, 1, 0:2] = prod[k, 1, 0:2] + xa[k, 0]
        xs(k, 4, prod.at[k, 1, pl.ds(0, 2)], right)
        x_in(k, 1)
        prod[k, 3, 2:4] = prod[k, 3, 2:4] + xa[k, 1]
        xs(k, 5, prod.at[k, 3, pl.ds(2, 2)], left)

    def x_sum(k):
        x_in(k, 3)
        x_in(k, 4)
        xr[k, 0:2] = prod[k, 0, 0:2] + xa[k, 4] + xa[k, 3]
        x_in(k, 2)
        x_in(k, 5)
        xr[k, 2:4] = prod[k, 0, 2:4] + xa[k, 2] + xa[k, 5]
        for d in (2, 1, 3):
            there = wrap(zh + d, 4)
            send(xr.at[k, there], zb.at[k, d - 1], z_s.at[k, d - 1], z_r.at[k, d - 1], at(x, y, there * 2 + zl, core))

    def z_sum(k):
        for d in range(3):
            arrived(zb.at[k, d], z_s.at[k, d], z_r.at[k, d])
        mask = fill[k, own_tile].astype(F32)
        block = -(xr[k, zh] + zb[k, 0] + zb[k, 1] + zb[k, 2]) * mask
        cb[:, k * W : (k + 1) * W] = block
        c_own[k, 0] = block[:, :HALF]
        c_own[k, 1] = block[:, HALF:]
        send(c_own.at[k, other], c_rec.at[k], c_s.at[k], c_r.at[k], partner)

    def local_term(k):
        t_h, t_l = t_high[k], t_low[k]
        arrived(c_rec.at[k], c_s.at[k], c_r.at[k])
        high, low = split(jnp.concatenate([c_own[k, core], c_rec[k]], axis=0))
        u[k] = three_pass(t_h, t_l, high, low).reshape(16, 16, HALF)

        @pl.loop(1, 16)
        def _(d):
            px, py = plane(d)
            copy(u.at[k, px * 4 + py], rs.at[k, d], p_s.at[k, d], p_r.at[k, d], at(px, py, z, core)).start()

    def plane_sum(k):
        total = u[k, slab]
        for d in range(1, 16):
            arrived(rs.at[k, d], p_s.at[k, d], p_r.at[k, d])
            total = total + rs[k, d]
        zs[k, z] = total

        @pl.loop(1, 8)
        def _(d):
            to = at(x, y, wrap(z + d, 8), core)
            copy(zs.at[k, z], zs.at[k, z], e_s.at[k, d], e_r.at[k, d], to).start()

    def line_sum(k):
        @pl.loop(1, 8)
        def _(d):
            arrived(zs.at[k, wrap(z - d, 8)], e_s.at[k, d], e_r.at[k, d])

        total = zs[k, 0]
        for n in range(1, 8):
            total = total + zs[k, n]
        g[k, core, slab] = d_slab[k] - total

        @pl.loop(1, 16)
        def _(d):
            px, py = plane(d)
            mine = g.at[k, core, slab]
            copy(mine, mine, q_s.at[k, d], q_r.at[k, d], at(px, py, z, core)).start()

    def spread(k):
        @pl.loop(1, 16)
        def _(d):
            px, py = wrap(x - lax.div(d, 4), 4), wrap(y - lax.rem(d, 4), 4)
            arrived(g.at[k, core, px * 4 + py], q_s.at[k, d], q_r.at[k, d])

        send(g.at[k, core], g.at[k, core], h_s.at[k], h_r.at[k], partner)

    def finish(k):
        arrived(g.at[k, other], h_s.at[k], h_r.at[k])
        dg[k, :, 0:HALF] = g[k, 0].reshape(W, HALF)
        dg[k, :, HALF:W] = g[k, 1].reshape(W, HALF)

    order = [
        (turned, 0), (turned, 1), (gather_a, 0), (turned, 2),
        (gather_b, 0), (gather_a, 1), (split_received, 0), (gather_c, 0),
        (gather_b, 1), (gather_a, 2), (gather_d, 0), (gather_c, 1),
        (gather_b, 2), (gather_e, 0), (x_one, 0), (x_two, 0),
        (gather_d, 1), (gather_c, 2), (gather_e, 1), (x_one, 1),
        (x_three, 0), (x_two, 1), (gather_d, 2), (gather_e, 2),
        (x_one, 2), (x_three, 1), (x_two, 2), (x_own, 0),
        (own_masks, 0), (x_own, 1), (x_sum, 0), (x_three, 2),
        (x_own, 2), (z_sum, 0), (local_term, 0), (x_sum, 1),
        (x_sum, 2), (z_sum, 1), (local_term, 1), (plane_sum, 0),
        (z_sum, 2), (local_term, 2), (plane_sum, 1), (line_sum, 0),
        (plane_sum, 2), (line_sum, 1), (spread, 0), (line_sum, 2),
        (spread, 1), (spread, 2), (finish, 0), (finish, 1),
        (finish, 2),
    ]
    for step, k in order:
        step(k)

    for out in sent:
        out.wait_send()
    for k in range(SIBS):

        @pl.loop(1, 16)
        def _(d):
            copy(u.at[k, 0], rs.at[k, d], p_s.at[k, d], p_r.at[k, d], partner).wait_send()
            copy(g.at[k, core, slab], g.at[k, core, slab], q_s.at[k, d], q_r.at[k, d], partner).wait_send()

        @pl.loop(1, 8)
        def _(d):
            copy(zs.at[k, z], zs.at[k, z], e_s.at[k, d], e_r.at[k, d], partner).wait_send()


def local(ancestor_inv, factor_rows, diagonal_inv, fill_list):
    vmem, dma = pltpu.VMEM, pltpu.SemaphoreType.DMA
    hbm = pl.BlockSpec(memory_space=pl.ANY)
    pairs = [(SIBS, 3), (SIBS, 4), (2,), (SIBS, 12), (SIBS, 6), (SIBS, 3), (SIBS,), (SIBS, 16), (SIBS, 8), (SIBS, 16), (SIBS,)]
    return pl.pallas_call(
        kernel,
        out_shape=(
            jax.ShapeDtypeStruct(factor_rows.shape, F32),
            jax.ShapeDtypeStruct(diagonal_inv.shape, F32),
        ),
        in_specs=[pl.BlockSpec(memory_space=pltpu.SMEM), hbm, hbm, hbm],
        out_specs=[pl.BlockSpec(memory_space=pltpu.VMEM)] * 2,
        scratch_shapes=[
            vmem((16, 64, 512), F32),
            vmem((16, 64, 512), F32),
            vmem((1024, 1024), BF16),
            vmem((1024, 1024), BF16),
            vmem((SIBS, 4, 2, 64, W), F32),
            vmem((SIBS, 4, 2, 64, W), F32),
            vmem((SIBS, 1024, W), BF16),
            vmem((SIBS, 1024, W), BF16),
            vmem((64, SIBS * W), F32),
            vmem((64, SIBS * W), F32),
            vmem((SIBS, W, 128), BF16),
            vmem((SIBS, W, 128), BF16),
            vmem((SIBS, 16, HALF), F32),
            vmem((SIBS, 4, 16, W), F32),
            vmem((SIBS, 4, 4, 64, W), F32),
            vmem((SIBS, 6, 2, 64, W), F32),
            vmem((SIBS, 4, 64, W), F32),
            vmem((SIBS, 3, 64, W), F32),
            vmem((SIBS, 2, 64, HALF), F32),
            vmem((SIBS, 64, HALF), F32),
            vmem((SIBS, 16, 16, HALF), F32),
            vmem((SIBS, 16, 16, HALF), F32),
            vmem((SIBS, 8, 16, HALF), F32),
            vmem((SIBS, 2, 16, 16, HALF), F32),
            dma((3,)),
        ]
        + [dma(shape) for shape in pairs for _ in range(2)],
        compiler_params=pltpu.CompilerParams(
            collective_id=0, has_side_effects=True, vmem_limit_bytes=52 * 1024 * 1024
        ),
    )(fill_list, factor_rows, ancestor_inv.reshape(16, 2, 64, 512), diagonal_inv)


def solution(mesh):
    placed = (P("row", "col"), P(("row", "col"), None), P(), P())
    return jax.shard_map(
        local, mesh=mesh, in_specs=placed, out_specs=(P(("row", "col"), None), P()), check_vma=False
    )
```

```python
import functools

import jax
import jax.numpy as jnp
from jax import lax
from jax.experimental import pallas as pl
from jax.experimental.pallas import tpu as pltpu
from jax.sharding import PartitionSpec as P

W = 256
SIBS = 3
CHUNKS = ((0, 0, 256), (1, 0, 256), (2, 0, 256))
HALF = 128
F32 = jnp.float32
BF16 = jnp.bfloat16


def split(v):
    high = v.astype(BF16)
    return high, (v - high.astype(F32)).astype(BF16)


def three_pass(a_high, a_low, b_high, b_low):
    dot = functools.partial(jnp.dot, preferred_element_type=F32)
    return dot(a_high, b_high) + (dot(a_high, b_low) + dot(a_low, b_high))


def kernel(
    fill, fac, a_in, cb, dg,
    a_own, a_rec, a_high, a_low, m_own, m_rec, m_high, m_low, f_all, t_high, t_low,
    turn, prod, xa, xr, zb, u_out, u_rec, u, rs, zs, g,
    local_sem, turn_s, turn_r, perm_s, perm_r, one_s, one_r, ag_s, ag_r, x_s, x_r, z_s, z_r, c_s, c_r,
    p_s, p_r, e_s, e_r, q_s, q_r, h_s, h_r,
):
    r = lax.axis_index("row")
    c = lax.axis_index("col")
    zl, y = lax.div(r, 4), lax.rem(r, 4)
    x, zh, core = lax.div(c, 8), lax.rem(lax.div(c, 2), 4), lax.rem(c, 2)
    z = zh * 2 + zl
    other = 1 - core
    slab = x * 4 + y

    def wrap(v, n):
        return lax.rem(v + n, n)

    def at(x_, y_, z_, core_):
        return (lax.rem(z_, 2) * 4 + y_, x_ * 8 + lax.div(z_, 2) * 2 + core_)

    def swap(v):
        return v + 1 - 2 * lax.rem(v, 2)

    partner = at(x, y, z, other)
    y_up, y_down = wrap(y + 1, 4), wrap(y - 1, 4)
    y_far = wrap(y + 2, 4)
    up, down = at(x, y_up, z, core), at(x, y_down, z, core)
    right, left = at(wrap(x + 1, 4), y, z, core), at(wrap(x - 1, 4), y, z, core)
    twin = at(x, y, zh * 2 + 1 - zl, core)
    part = lax.div(zh, 2) * 2 + core

    def target(y_from):
        z_to = (2 * lax.rem(y_from, 2) + lax.div(x, 2)) * 2 + 1 - lax.rem(zh, 2)
        return at(2 * zl + lax.div(y_from, 2), y, z_to, lax.rem(x, 2))

    def source(n):
        z_from = ((n // 2) * 2 + 1 - zl) * 2 + lax.div(x, 2)
        return at(2 * lax.rem(zh, 2) + core, y, z_from, n % 2)

    def plane(d):
        return wrap(x + lax.div(d, 4), 4), wrap(y + lax.rem(d, 4), 4)

    barrier = pltpu.get_barrier_semaphore()

    def hello(device):
        pl.semaphore_signal(barrier, inc=1, device_id=device, device_id_type=pl.DeviceIdType.MESH)

    @pl.loop(1, 16)
    def _(d):
        px, py = plane(d)
        hello(at(px, py, z, core))

    @pl.loop(1, 8)
    def _(d):
        hello(at(x, y, wrap(z + d, 8), core))

    hello(partner)
    for n in range(4):
        hello(target(n))
        hello(source(n))

    own_rows = pltpu.make_async_copy(a_in.at[:, core], a_own, local_sem.at[0])
    own_rows.start()
    own_factor = pltpu.make_async_copy(fac, f_all.at[zh], local_sem.at[1])
    own_factor.start()
    def split_rows(src, column):
        @pl.loop(0, 16)
        def _(i):
            rows = pl.ds(pl.multiple_of(i * 64, 64), 64)
            high, low = split(src[i])
            a_high[rows, column : column + 512] = high
            a_low[rows, column : column + 512] = low

    own_rows.wait()
    split_rows(a_own, 0)
    pl.semaphore_wait(barrier, 31)

    sent = []

    def copy(src, dst, ssem, rsem, device):
        return pltpu.make_async_remote_copy(
            src_ref=src, dst_ref=dst, send_sem=ssem, recv_sem=rsem,
            device_id=device, device_id_type=pl.DeviceIdType.MESH,
        )

    def send(src, dst, ssem, rsem, device):
        out = copy(src, dst, ssem, rsem, device)
        out.start()
        sent.append(out)

    def arrived(dst, ssem, rsem):
        copy(dst, dst, ssem, rsem, partner).wait_recv()


    def columns(i):
        k, first, width = CHUNKS[i]
        return k, pl.ds(first, width), first, width

    def quarter(i, n):
        k, _, first, width = columns(i)
        return fac.at[pl.ds(pl.multiple_of(n * 16, 16), 16), pl.ds(k * W + first, width)]

    def forward(i, n, y_from, src):
        k, cut, _, _ = columns(i)
        landing = m_own.at[k, y, 1 - lax.rem(zh, 2), pl.ds(pl.multiple_of(part * 16, 16), 16), cut]
        send(src, landing, perm_s.at[i, n], perm_r.at[i, part], target(y_from))

    for i in range(len(CHUNKS)):
        k, cut, _, _ = columns(i)
        for d in (2, 1, 3):
            y_to = wrap(y + d, 4)
            to = at(x, y_to, z, core)
            send(quarter(i, y_to), turn.at[k, y, :, cut], turn_s.at[i, d - 1], turn_r.at[i, d - 1], to)
        forward(i, 0, y, quarter(i, y))
    send(a_in.at[:, other], a_rec, one_s.at[0], one_r.at[0], partner)

    def split_received(_):
        arrived(a_rec, one_s.at[0], one_r.at[0])
        split_rows(a_rec, 512)

    def ag(i, n, src, dst, device):
        send(src, dst, ag_s.at[i, n], ag_r.at[i, n], device)

    def ag_in(i, n, dst):
        arrived(dst, ag_s.at[i, n], ag_r.at[i, n])

    def one(ref, i, m, half):
        k, cut, _, _ = columns(i)
        return ref.at[k, m, half, :, cut]

    def both(ref, i, m):
        k, cut, _, _ = columns(i)
        return ref.at[k, m, :, :, cut]

    def turned(i):
        k, cut, _, _ = columns(i)
        for d in (1, 3, 2):
            y_from = wrap(y - d, 4)
            landed = turn.at[k, y_from, :, cut]
            arrived(landed, turn_s.at[i, d - 1], turn_r.at[i, d - 1])
            forward(i, d, y_from, landed)

    def gather_a(i):
        k, cut, _, _ = columns(i)
        own = one(m_own, i, y, zl)
        for n in range(4):
            arrived(m_own.at[k, y, zl, pl.ds(n * 16, 16), cut], perm_s.at[i, n], perm_r.at[i, n])
        ag(i, 0, own, own, twin)
        ag(i, 1, own, own, up)
        ag(i, 2, own, own, down)
        ag(i, 3, own, one(m_rec, i, y, zl), partner)

    def gather_b(i):
        own = one(m_own, i, y, 1 - zl)
        ag_in(i, 0, own)
        ag(i, 4, own, own, up)
        ag(i, 5, own, own, down)
        ag(i, 6, own, one(m_rec, i, y, 1 - zl), partner)

    def gather_c(i):
        low = one(m_own, i, y_down, zl)
        ag_in(i, 1, low)
        ag(i, 7, low, low, up)
        high = one(m_own, i, y_up, 1 - zl)
        ag_in(i, 5, high)
        ag(i, 8, high, high, down)

    def gather_d(i):
        ag_in(i, 4, one(m_own, i, y_down, 1 - zl))
        ag(i, 9, both(m_own, i, y_down), both(m_rec, i, y_down), partner)
        ag_in(i, 2, one(m_own, i, y_up, zl))
        ag(i, 10, both(m_own, i, y_up), both(m_rec, i, y_up), partner)
        ag_in(i, 7, one(m_own, i, y_far, zl))
        ag_in(i, 8, one(m_own, i, y_far, 1 - zl))
        ag(i, 11, both(m_own, i, y_far), both(m_rec, i, y_far), partner)

    def split_pieces(i, src, column, start):
        k, _, first, width = columns(i)
        cut = slice(first, first + width)
        for n in range(4):
            mask = fill[k, 2 * column + n // 2].astype(F32)
            for half in range(2):
                piece = (n // 2) * 4 + (1 - half) * 2 + n % 2
                for m in range(4):
                    row = start + piece * 64 + m * 16
                    high, low = split(src[k, m, half, n * 16 : n * 16 + 16, cut] * mask)
                    m_high[k, row : row + 16, cut] = high
                    m_low[k, row : row + 16, cut] = low

    def gather_e(i):
        split_pieces(i, m_own, c, 0)
        ag_in(i, 3, one(m_rec, i, y, zl))
        ag_in(i, 6, one(m_rec, i, y, 1 - zl))
        ag_in(i, 9, both(m_rec, i, y_down))
        ag_in(i, 10, both(m_rec, i, y_up))
        ag_in(i, 11, both(m_rec, i, y_far))
        split_pieces(i, m_rec, swap(c), 512)

    own_tile = r * 8 + lax.div(c, 4)

    def share_factor(_):
        for d in (2, 1, 3):
            to = at(x, y, wrap(zh + d, 4) * 2 + zl, core)
            send(fac, f_all.at[zh], one_s.at[d], one_r.at[d], to)

    def own_masks(_):
        own_factor.wait()
        for d in range(1, 4):
            arrived(f_all.at[wrap(zh - d, 4)], one_s.at[d], one_r.at[d])
        for k in range(SIBS):
            for n in range(4):
                mask = fill[k, r * 8 + x * 2 + n // 2].astype(F32)
                high, low = split((f_all[n, :, k * W : (k + 1) * W] * (mask * mask)).T)
                t_high[k, :, n * 64 : (n + 1) * 64] = high
                t_low[k, :, n * 64 : (n + 1) * 64] = low

    def multiply(i, away):
        k, _, first, width = columns(i)
        cut = slice(first, first + width)
        rows = pl.ds(pl.multiple_of(wrap(x + away, 4) * 256, 256), 256)
        result = three_pass(a_high[rows, :], a_low[rows, :], m_high[k, :, cut], m_low[k, :, cut])
        prod[k, away, :, :, cut] = result.reshape(4, 64, width)

    def x_own(i):
        multiply(i, 0)

    def xs(i, n, away, pair, device):
        k, cut, _, _ = columns(i)
        send(prod.at[k, away, pl.ds(pair, 2), :, cut], xa.at[k, n, :, :, cut], x_s.at[i, n], x_r.at[i, n], device)

    def x_in(i, n):
        k, cut, _, _ = columns(i)
        arrived(xa.at[k, n, :, :, cut], x_s.at[i, n], x_r.at[i, n])

    def x_one(i):
        multiply(i, 2)
        xs(i, 0, 2, 0, right)
        xs(i, 1, 2, 2, left)

    def x_two(i):
        multiply(i, 1)
        xs(i, 2, 1, 2, right)
        multiply(i, 3)
        xs(i, 3, 3, 0, left)

    def x_three(i):
        k, _, first, width = columns(i)
        cut = slice(first, first + width)
        x_in(i, 0)
        prod[k, 1, 0:2, :, cut] = prod[k, 1, 0:2, :, cut] + xa[k, 0, :, :, cut]
        xs(i, 4, 1, 0, right)
        x_in(i, 1)
        prod[k, 3, 2:4, :, cut] = prod[k, 3, 2:4, :, cut] + xa[k, 1, :, :, cut]
        xs(i, 5, 3, 2, left)

    def x_sum(i):
        k, lanes, first, width = columns(i)
        cut = slice(first, first + width)
        x_in(i, 3)
        x_in(i, 4)
        xr[k, 0:2, :, cut] = prod[k, 0, 0:2, :, cut] + xa[k, 4, :, :, cut] + xa[k, 3, :, :, cut]
        x_in(i, 2)
        x_in(i, 5)
        xr[k, 2:4, :, cut] = prod[k, 0, 2:4, :, cut] + xa[k, 2, :, :, cut] + xa[k, 5, :, :, cut]
        for d in (2, 1, 3):
            there = wrap(zh + d, 4)
            to = at(x, y, there * 2 + zl, core)
            send(xr.at[k, there, :, lanes], zb.at[k, d - 1, :, lanes], z_s.at[i, d - 1], z_r.at[i, d - 1], to)

    def z_sum(i):
        k, lanes, first, width = columns(i)
        cut = slice(first, first + width)
        for d in range(3):
            arrived(zb.at[k, d, :, lanes], z_s.at[i, d], z_r.at[i, d])
        mask = fill[k, own_tile].astype(F32)
        block = -(xr[k, zh, :, cut] + zb[k, 0, :, cut] + zb[k, 1, :, cut] + zb[k, 2, :, cut]) * mask
        cb[:, k * W + first : k * W + first + width] = block

    def local_term(i):
        k, lanes, first, width = columns(i)
        cut = slice(first, first + width)
        high, low = split(xr[k, :, :, cut].reshape(W, width))
        whole = three_pass(t_high[k], t_low[k], high, low)
        u_out[k, 0, :, :, cut] = whole[:HALF].reshape(16, 8, width)
        u_out[k, 1, :, :, cut] = whole[HALF:].reshape(16, 8, width)
        send(u_out.at[k, other, :, :, lanes], u_rec.at[k, :, :, lanes], c_s.at[i], c_r.at[i], partner)

    def chip_term(i):
        k, lanes, first, width = columns(i)
        cut = slice(first, first + width)
        arrived(u_rec.at[k, :, :, lanes], c_s.at[i], c_r.at[i])
        u[k, :, :, cut] = u_out[k, core, :, :, cut] + u_rec[k, :, :, cut]

        @pl.loop(1, 16)
        def _(d):
            px, py = plane(d)
            src, dst = u.at[k, px * 4 + py, :, lanes], rs.at[k, d, :, lanes]
            copy(src, dst, p_s.at[i, d], p_r.at[i, d], at(px, py, z, core)).start()

    def plane_sum(i):
        k, lanes, first, width = columns(i)
        cut = slice(first, first + width)
        total = u[k, slab, :, cut]
        for d in range(1, 16):
            arrived(rs.at[k, d, :, lanes], p_s.at[i, d], p_r.at[i, d])
            total = total + rs[k, d, :, cut]
        zs[k, z, :, cut] = total

        @pl.loop(1, 8)
        def _(d):
            mine = zs.at[k, z, :, lanes]
            copy(mine, mine, e_s.at[i, d], e_r.at[i, d], at(x, y, wrap(z + d, 8), core)).start()

    def line_sum(i):
        k, lanes, first, width = columns(i)
        cut = slice(first, first + width)

        @pl.loop(1, 8)
        def _(d):
            arrived(zs.at[k, wrap(z - d, 8), :, lanes], e_s.at[i, d], e_r.at[i, d])

        total = zs[k, 0, :, cut]
        for n in range(1, 8):
            total = total + zs[k, n, :, cut]
        g[k, core, slab, :, cut] = total

        @pl.loop(1, 16)
        def _(d):
            px, py = plane(d)
            mine = g.at[k, core, slab, :, lanes]
            copy(mine, mine, q_s.at[i, d], q_r.at[i, d], at(px, py, z, core)).start()

    def spread(i):
        k, lanes, _, _ = columns(i)

        @pl.loop(1, 16)
        def _(d):
            px, py = wrap(x - lax.div(d, 4), 4), wrap(y - lax.rem(d, 4), 4)
            arrived(g.at[k, core, px * 4 + py, :, lanes], q_s.at[i, d], q_r.at[i, d])

        mine = g.at[k, core, :, :, lanes]
        send(mine, mine, h_s.at[i], h_r.at[i], partner)

    def finish(i):
        k, lanes, first, width = columns(i)
        cut = slice(first, first + width)
        arrived(g.at[k, other, :, :, lanes], h_s.at[i], h_r.at[i])
        for n in range(2):
            dg[k, n * HALF : (n + 1) * HALF, cut] = g[k, n, :, :, cut].reshape(HALF, width)

    order = [
        (turned, 0), (turned, 1), (gather_a, 0), (turned, 2),
        (gather_b, 0), (gather_a, 1), (split_received, 0), (gather_c, 0),
        (gather_b, 1), (gather_a, 2), (gather_d, 0), (gather_c, 1),
        (gather_b, 2), (share_factor, 0), (gather_e, 0), (x_one, 0),
        (x_two, 0), (gather_d, 1), (gather_c, 2), (gather_e, 1),
        (x_one, 1), (x_three, 0), (x_two, 1), (gather_d, 2),
        (gather_e, 2), (x_one, 2), (x_three, 1), (x_two, 2),
        (x_own, 0), (x_own, 1), (x_sum, 0), (x_three, 2),
        (x_own, 2), (own_masks, 0), (local_term, 0), (chip_term, 0),
        (z_sum, 0), (x_sum, 1), (local_term, 1), (chip_term, 1),
        (x_sum, 2), (local_term, 2), (plane_sum, 0), (chip_term, 2),
        (z_sum, 1), (plane_sum, 1), (line_sum, 0), (z_sum, 2),
        (plane_sum, 2), (line_sum, 1), (spread, 0), (line_sum, 2),
        (spread, 1), (spread, 2), (finish, 0), (finish, 1),
        (finish, 2),
    ]
    for step, i in order:
        step(i)

    for out in sent:
        out.wait_send()
    for i in range(len(CHUNKS)):
        k, lanes, _, _ = columns(i)

        @pl.loop(1, 16)
        def _(d):
            copy(u.at[k, 0, :, lanes], rs.at[k, d, :, lanes], p_s.at[i, d], p_r.at[i, d], partner).wait_send()
            mine = g.at[k, core, slab, :, lanes]
            copy(mine, mine, q_s.at[i, d], q_r.at[i, d], partner).wait_send()

        @pl.loop(1, 8)
        def _(d):
            mine = zs.at[k, z, :, lanes]
            copy(mine, mine, e_s.at[i, d], e_r.at[i, d], partner).wait_send()


def local(ancestor_inv, factor_rows, diagonal_inv, fill_list):
    vmem, dma = pltpu.VMEM, pltpu.SemaphoreType.DMA
    hbm = pl.BlockSpec(memory_space=pl.ANY)
    n = len(CHUNKS)
    pairs = [(n, 3), (n, 4), (4,), (n, 12), (n, 6), (n, 3), (n,), (n, 16), (n, 8), (n, 16), (n,)]
    block, update = pl.pallas_call(
        kernel,
        out_shape=(
            jax.ShapeDtypeStruct(factor_rows.shape, F32),
            jax.ShapeDtypeStruct(diagonal_inv.shape, F32),
        ),
        in_specs=[pl.BlockSpec(memory_space=pltpu.SMEM), hbm, hbm],
        out_specs=[pl.BlockSpec(memory_space=pltpu.VMEM)] * 2,
        scratch_shapes=[
            vmem((16, 64, 512), F32),
            vmem((16, 64, 512), F32),
            vmem((1024, 1024), BF16),
            vmem((1024, 1024), BF16),
            vmem((SIBS, 4, 2, 64, W), F32),
            vmem((SIBS, 4, 2, 64, W), F32),
            vmem((SIBS, 1024, W), BF16),
            vmem((SIBS, 1024, W), BF16),
            vmem((4, 64, SIBS * W), F32),
            vmem((SIBS, W, W), BF16),
            vmem((SIBS, W, W), BF16),
            vmem((SIBS, 4, 16, W), F32),
            vmem((SIBS, 4, 4, 64, W), F32),
            vmem((SIBS, 6, 2, 64, W), F32),
            vmem((SIBS, 4, 64, W), F32),
            vmem((SIBS, 3, 64, W), F32),
            vmem((SIBS, 2, 16, 8, W), F32),
            vmem((SIBS, 16, 8, W), F32),
            vmem((SIBS, 16, 8, W), F32),
            vmem((SIBS, 16, 8, W), F32),
            vmem((SIBS, 8, 8, W), F32),
            vmem((SIBS, 2, 16, 8, W), F32),
            dma((2,)),
        ]
        + [dma(shape) for shape in pairs for _ in range(2)],
        compiler_params=pltpu.CompilerParams(
            collective_id=0, has_side_effects=True, vmem_limit_bytes=52 * 1024 * 1024
        ),
    )(fill_list, factor_rows, ancestor_inv.reshape(16, 2, 64, 512))
    return block, diagonal_inv + update


def solution(mesh):
    placed = (P("row", "col"), P(("row", "col"), None), P(), P())
    return jax.shard_map(
        local, mesh=mesh, in_specs=placed, out_specs=(P(("row", "col"), None), P()), check_vma=False
    )
```

```python
import functools

import jax
import jax.numpy as jnp
from jax import lax
from jax.experimental import pallas as pl
from jax.experimental.pallas import tpu as pltpu
from jax.sharding import PartitionSpec as P

W = 256
SIBS = 3
CHUNKS = ((0, 0, 256), (1, 0, 256), (2, 0, 256))
HALF = 128
F32 = jnp.float32
BF16 = jnp.bfloat16


def split(v):
    high = v.astype(BF16)
    return high, (v - high.astype(F32)).astype(BF16)


def three_pass(a_high, a_low, b_high, b_low):
    dot = functools.partial(jnp.dot, preferred_element_type=F32)
    return dot(a_high, b_high) + (dot(a_high, b_low) + dot(a_low, b_high))


def kernel(
    fill, fac, a_in, cb, dg,
    a_own, a_rec, a_high, a_low, m_own, m_rec, m_high, m_low, f_all, t_high, t_low,
    turn, prod, xa, xr, zb, u_out, u_rec, u, rs, zs, g,
    local_sem, turn_s, turn_r, perm_s, perm_r, one_s, one_r, ag_s, ag_r, x_s, x_r, z_s, z_r, c_s, c_r,
    p_s, p_r, e_s, e_r, q_s, q_r, h_s, h_r,
):
    r = lax.axis_index("row")
    c = lax.axis_index("col")
    zl, y = lax.div(r, 4), lax.rem(r, 4)
    x, zh, core = lax.div(c, 8), lax.rem(lax.div(c, 2), 4), lax.rem(c, 2)
    z = zh * 2 + zl
    other = 1 - core
    slab = x * 4 + y

    def wrap(v, n):
        return lax.rem(v + n, n)

    def at(x_, y_, z_, core_):
        return (lax.rem(z_, 2) * 4 + y_, x_ * 8 + lax.div(z_, 2) * 2 + core_)

    def swap(v):
        return v + 1 - 2 * lax.rem(v, 2)

    partner = at(x, y, z, other)
    y_up, y_down = wrap(y + 1, 4), wrap(y - 1, 4)
    y_far = wrap(y + 2, 4)
    up, down = at(x, y_up, z, core), at(x, y_down, z, core)
    right, left = at(wrap(x + 1, 4), y, z, core), at(wrap(x - 1, 4), y, z, core)
    twin = at(x, y, zh * 2 + 1 - zl, core)
    part = lax.div(zh, 2) * 2 + core

    def target(y_from):
        z_to = (2 * lax.rem(y_from, 2) + lax.div(x, 2)) * 2 + 1 - lax.rem(zh, 2)
        return at(2 * zl + lax.div(y_from, 2), y, z_to, lax.rem(x, 2))

    def source(n):
        z_from = ((n // 2) * 2 + 1 - zl) * 2 + lax.div(x, 2)
        return at(2 * lax.rem(zh, 2) + core, y, z_from, n % 2)

    def plane(d):
        return wrap(x + lax.div(d, 4), 4), wrap(y + lax.rem(d, 4), 4)

    barrier = pltpu.get_barrier_semaphore()

    def hello(device):
        pl.semaphore_signal(barrier, inc=1, device_id=device, device_id_type=pl.DeviceIdType.MESH)

    @pl.loop(1, 16)
    def _(d):
        px, py = plane(d)
        hello(at(px, py, z, core))

    @pl.loop(1, 8)
    def _(d):
        hello(at(x, y, wrap(z + d, 8), core))

    hello(partner)
    for n in range(4):
        hello(target(n))
        hello(source(n))

    own_rows = pltpu.make_async_copy(a_in.at[:, core], a_own, local_sem.at[0])
    own_rows.start()
    own_factor = pltpu.make_async_copy(fac, f_all.at[zh], local_sem.at[1])
    own_factor.start()
    def split_rows(src, column):
        @pl.loop(0, 16)
        def _(i):
            rows = pl.ds(pl.multiple_of(i * 64, 64), 64)
            high, low = split(src[i])
            a_high[rows, column : column + 512] = high
            a_low[rows, column : column + 512] = low

    own_rows.wait()
    split_rows(a_own, 0)
    pl.semaphore_wait(barrier, 31)

    sent = []

    def copy(src, dst, ssem, rsem, device):
        return pltpu.make_async_remote_copy(
            src_ref=src, dst_ref=dst, send_sem=ssem, recv_sem=rsem,
            device_id=device, device_id_type=pl.DeviceIdType.MESH,
        )

    def send(src, dst, ssem, rsem, device):
        out = copy(src, dst, ssem, rsem, device)
        out.start()
        sent.append(out)

    def arrived(dst, ssem, rsem):
        copy(dst, dst, ssem, rsem, partner).wait_recv()


    def columns(i):
        k, first, width = CHUNKS[i]
        return k, pl.ds(first, width), first, width

    def quarter(i, n):
        k, _, first, width = columns(i)
        return fac.at[pl.ds(pl.multiple_of(n * 16, 16), 16), pl.ds(k * W + first, width)]

    def forward(i, n, y_from, src):
        k, cut, _, _ = columns(i)
        landing = m_own.at[k, y, 1 - lax.rem(zh, 2), pl.ds(pl.multiple_of(part * 16, 16), 16), cut]
        send(src, landing, perm_s.at[i, n], perm_r.at[i, part], target(y_from))

    for i in range(len(CHUNKS)):
        k, cut, _, _ = columns(i)
        for d in (2, 1, 3):
            y_to = wrap(y + d, 4)
            to = at(x, y_to, z, core)
            send(quarter(i, y_to), turn.at[k, y, :, cut], turn_s.at[i, d - 1], turn_r.at[i, d - 1], to)
        forward(i, 0, y, quarter(i, y))
    send(a_in.at[:, other], a_rec, one_s.at[0], one_r.at[0], partner)

    def split_received(_):
        arrived(a_rec, one_s.at[0], one_r.at[0])
        split_rows(a_rec, 512)

    def ag(i, n, src, dst, device):
        send(src, dst, ag_s.at[i, n], ag_r.at[i, n], device)

    def ag_in(i, n, dst):
        arrived(dst, ag_s.at[i, n], ag_r.at[i, n])

    def one(ref, i, m, half):
        k, cut, _, _ = columns(i)
        return ref.at[k, m, half, :, cut]

    def both(ref, i, m):
        k, cut, _, _ = columns(i)
        return ref.at[k, m, :, :, cut]

    def turned(i):
        k, cut, _, _ = columns(i)
        for d in (1, 3, 2):
            y_from = wrap(y - d, 4)
            landed = turn.at[k, y_from, :, cut]
            arrived(landed, turn_s.at[i, d - 1], turn_r.at[i, d - 1])
            forward(i, d, y_from, landed)

    def gather_a(i):
        k, cut, _, _ = columns(i)
        own = one(m_own, i, y, zl)
        for n in range(4):
            arrived(m_own.at[k, y, zl, pl.ds(n * 16, 16), cut], perm_s.at[i, n], perm_r.at[i, n])
        ag(i, 0, own, own, twin)
        ag(i, 1, own, own, up)
        ag(i, 2, own, own, down)
        ag(i, 3, own, one(m_rec, i, y, zl), partner)

    def gather_b(i):
        own = one(m_own, i, y, 1 - zl)
        ag_in(i, 0, own)
        ag(i, 4, own, own, up)
        ag(i, 5, own, own, down)
        ag(i, 6, own, one(m_rec, i, y, 1 - zl), partner)

    def gather_c(i):
        low = one(m_own, i, y_down, zl)
        ag_in(i, 1, low)
        ag(i, 7, low, low, up)
        high = one(m_own, i, y_up, 1 - zl)
        ag_in(i, 5, high)
        ag(i, 8, high, high, down)

    def gather_d(i):
        ag_in(i, 4, one(m_own, i, y_down, 1 - zl))
        ag(i, 9, both(m_own, i, y_down), both(m_rec, i, y_down), partner)
        ag_in(i, 2, one(m_own, i, y_up, zl))
        ag(i, 10, both(m_own, i, y_up), both(m_rec, i, y_up), partner)
        ag_in(i, 7, one(m_own, i, y_far, zl))
        ag_in(i, 8, one(m_own, i, y_far, 1 - zl))
        ag(i, 11, both(m_own, i, y_far), both(m_rec, i, y_far), partner)

    def split_pieces(i, src, column, start):
        k, _, first, width = columns(i)
        cut = slice(first, first + width)
        for n in range(4):
            mask = fill[k, 2 * column + n // 2].astype(F32)
            for half in range(2):
                piece = (n // 2) * 4 + (1 - half) * 2 + n % 2
                for m in range(4):
                    row = start + piece * 64 + m * 16
                    high, low = split(src[k, m, half, n * 16 : n * 16 + 16, cut] * mask)
                    m_high[k, row : row + 16, cut] = high
                    m_low[k, row : row + 16, cut] = low

    def gather_e(i):
        split_pieces(i, m_own, c, 0)
        ag_in(i, 3, one(m_rec, i, y, zl))
        ag_in(i, 6, one(m_rec, i, y, 1 - zl))
        ag_in(i, 9, both(m_rec, i, y_down))
        ag_in(i, 10, both(m_rec, i, y_up))
        ag_in(i, 11, both(m_rec, i, y_far))
        split_pieces(i, m_rec, swap(c), 512)

    own_tile = r * 8 + lax.div(c, 4)

    def share_factor(_):
        for d in (2, 1, 3):
            to = at(x, y, wrap(zh + d, 4) * 2 + zl, core)
            send(fac, f_all.at[zh], one_s.at[d], one_r.at[d], to)

    def own_masks(_):
        own_factor.wait()
        for d in range(1, 4):
            arrived(f_all.at[wrap(zh - d, 4)], one_s.at[d], one_r.at[d])
        for k in range(SIBS):
            for n in range(4):
                mask = fill[k, r * 8 + x * 2 + n // 2].astype(F32)
                high, low = split((f_all[n, :, k * W : (k + 1) * W] * (mask * mask)).T)
                t_high[k, :, n * 64 : (n + 1) * 64] = high
                t_low[k, :, n * 64 : (n + 1) * 64] = low

    def multiply(i, away):
        k, _, first, width = columns(i)
        cut = slice(first, first + width)
        rows = pl.ds(pl.multiple_of(wrap(x + away, 4) * 256, 256), 256)
        result = three_pass(a_high[rows, :], a_low[rows, :], m_high[k, :, cut], m_low[k, :, cut])
        prod[k, away, :, :, cut] = result.reshape(4, 64, width)

    def x_own(i):
        multiply(i, 0)

    def xs(i, n, away, pair, device):
        k, cut, _, _ = columns(i)
        send(prod.at[k, away, pl.ds(pair, 2), :, cut], xa.at[k, n, :, :, cut], x_s.at[i, n], x_r.at[i, n], device)

    def x_in(i, n):
        k, cut, _, _ = columns(i)
        arrived(xa.at[k, n, :, :, cut], x_s.at[i, n], x_r.at[i, n])

    def x_one(i):
        multiply(i, 2)
        xs(i, 0, 2, 0, right)
        xs(i, 1, 2, 2, left)

    def x_two(i):
        multiply(i, 1)
        xs(i, 2, 1, 2, right)
        multiply(i, 3)
        xs(i, 3, 3, 0, left)

    def x_three(i):
        k, _, first, width = columns(i)
        cut = slice(first, first + width)
        x_in(i, 0)
        prod[k, 1, 0:2, :, cut] = prod[k, 1, 0:2, :, cut] + xa[k, 0, :, :, cut]
        xs(i, 4, 1, 0, right)
        x_in(i, 1)
        prod[k, 3, 2:4, :, cut] = prod[k, 3, 2:4, :, cut] + xa[k, 1, :, :, cut]
        xs(i, 5, 3, 2, left)

    def x_sum(i):
        k, lanes, first, width = columns(i)
        cut = slice(first, first + width)
        x_in(i, 3)
        x_in(i, 4)
        xr[k, 0:2, :, cut] = prod[k, 0, 0:2, :, cut] + xa[k, 4, :, :, cut] + xa[k, 3, :, :, cut]
        x_in(i, 2)
        x_in(i, 5)
        xr[k, 2:4, :, cut] = prod[k, 0, 2:4, :, cut] + xa[k, 2, :, :, cut] + xa[k, 5, :, :, cut]
        for d in (2, 1, 3):
            there = wrap(zh + d, 4)
            to = at(x, y, there * 2 + zl, core)
            send(xr.at[k, there, :, lanes], zb.at[k, d - 1, :, lanes], z_s.at[i, d - 1], z_r.at[i, d - 1], to)

    def z_sum(i):
        k, lanes, first, width = columns(i)
        cut = slice(first, first + width)
        for d in range(3):
            arrived(zb.at[k, d, :, lanes], z_s.at[i, d], z_r.at[i, d])
        mask = fill[k, own_tile].astype(F32)
        block = -(xr[k, zh, :, cut] + zb[k, 0, :, cut] + zb[k, 1, :, cut] + zb[k, 2, :, cut]) * mask
        cb[:, k * W + first : k * W + first + width] = block

    def local_term(i):
        k, lanes, first, width = columns(i)
        cut = slice(first, first + width)
        high, low = split(xr[k, :, :, cut].reshape(W, width))
        whole = three_pass(t_high[k], t_low[k], high, low)
        u_out[k, 0, :, :, cut] = whole[:HALF].reshape(16, 8, width)
        u_out[k, 1, :, :, cut] = whole[HALF:].reshape(16, 8, width)
        send(u_out.at[k, other, :, :, lanes], u_rec.at[k, :, :, lanes], c_s.at[i], c_r.at[i], partner)

    def chip_term(i):
        k, lanes, first, width = columns(i)
        cut = slice(first, first + width)
        arrived(u_rec.at[k, :, :, lanes], c_s.at[i], c_r.at[i])
        u[k, :, :, cut] = u_out[k, core, :, :, cut] + u_rec[k, :, :, cut]

        @pl.loop(1, 16)
        def _(d):
            px, py = plane(d)
            src, dst = u.at[k, px * 4 + py, :, lanes], rs.at[k, d, :, lanes]
            copy(src, dst, p_s.at[i, d], p_r.at[i, d], at(px, py, z, core)).start()

    def plane_sum(i):
        k, lanes, first, width = columns(i)
        cut = slice(first, first + width)
        total = u[k, slab, :, cut]
        for d in range(1, 16):
            arrived(rs.at[k, d, :, lanes], p_s.at[i, d], p_r.at[i, d])
            total = total + rs[k, d, :, cut]
        zs[k, z, :, cut] = total

        @pl.loop(1, 8)
        def _(d):
            mine = zs.at[k, z, :, lanes]
            copy(mine, mine, e_s.at[i, d], e_r.at[i, d], at(x, y, wrap(z + d, 8), core)).start()

    def line_sum(i):
        k, lanes, first, width = columns(i)
        cut = slice(first, first + width)

        @pl.loop(1, 8)
        def _(d):
            arrived(zs.at[k, wrap(z - d, 8), :, lanes], e_s.at[i, d], e_r.at[i, d])

        total = zs[k, 0, :, cut]
        for n in range(1, 8):
            total = total + zs[k, n, :, cut]
        g[k, core, slab, :, cut] = total

        @pl.loop(1, 16)
        def _(d):
            px, py = plane(d)
            mine = g.at[k, core, slab, :, lanes]
            copy(mine, mine, q_s.at[i, d], q_r.at[i, d], at(px, py, z, core)).start()

    def spread(i):
        k, lanes, _, _ = columns(i)

        @pl.loop(1, 16)
        def _(d):
            px, py = wrap(x - lax.div(d, 4), 4), wrap(y - lax.rem(d, 4), 4)
            arrived(g.at[k, core, px * 4 + py, :, lanes], q_s.at[i, d], q_r.at[i, d])

        mine = g.at[k, core, :, :, lanes]
        send(mine, mine, h_s.at[i], h_r.at[i], partner)

    def finish(i):
        k, lanes, first, width = columns(i)
        cut = slice(first, first + width)
        arrived(g.at[k, other, :, :, lanes], h_s.at[i], h_r.at[i])
        for n in range(2):
            dg[k, n * HALF : (n + 1) * HALF, cut] = g[k, n, :, :, cut].reshape(HALF, width)

    order = [
        (turned, 0), (turned, 1), (gather_a, 0), (turned, 2),
        (gather_b, 0), (gather_a, 1), (split_received, 0), (gather_c, 0),
        (gather_b, 1), (gather_a, 2), (gather_d, 0), (gather_c, 1),
        (gather_b, 2), (share_factor, 0), (gather_e, 0), (x_one, 0),
        (x_two, 0), (gather_d, 1), (gather_c, 2), (gather_e, 1),
        (x_one, 1), (x_three, 0), (x_two, 1), (gather_d, 2),
        (gather_e, 2), (x_one, 2), (x_three, 1), (x_two, 2),
        (x_own, 0), (x_own, 1), (x_sum, 0), (x_three, 2),
        (x_own, 2), (x_sum, 1), (own_masks, 0), (local_term, 0),
        (local_term, 1), (chip_term, 0), (chip_term, 1), (x_sum, 2),
        (local_term, 2), (z_sum, 0), (chip_term, 2), (plane_sum, 0),
        (plane_sum, 1), (z_sum, 1), (line_sum, 0), (plane_sum, 2),
        (z_sum, 2), (line_sum, 1), (spread, 0), (line_sum, 2),
        (spread, 1), (spread, 2), (finish, 0), (finish, 1),
        (finish, 2),
    ]
    for step, i in order:
        step(i)

    for out in sent:
        out.wait_send()
    for i in range(len(CHUNKS)):
        k, lanes, _, _ = columns(i)

        @pl.loop(1, 16)
        def _(d):
            copy(u.at[k, 0, :, lanes], rs.at[k, d, :, lanes], p_s.at[i, d], p_r.at[i, d], partner).wait_send()
            mine = g.at[k, core, slab, :, lanes]
            copy(mine, mine, q_s.at[i, d], q_r.at[i, d], partner).wait_send()

        @pl.loop(1, 8)
        def _(d):
            mine = zs.at[k, z, :, lanes]
            copy(mine, mine, e_s.at[i, d], e_r.at[i, d], partner).wait_send()


def local(ancestor_inv, factor_rows, diagonal_inv, fill_list):
    vmem, dma = pltpu.VMEM, pltpu.SemaphoreType.DMA
    hbm = pl.BlockSpec(memory_space=pl.ANY)
    n = len(CHUNKS)
    pairs = [(n, 3), (n, 4), (4,), (n, 12), (n, 6), (n, 3), (n,), (n, 16), (n, 8), (n, 16), (n,)]
    block, update = pl.pallas_call(
        kernel,
        out_shape=(
            jax.ShapeDtypeStruct(factor_rows.shape, F32),
            jax.ShapeDtypeStruct(diagonal_inv.shape, F32),
        ),
        in_specs=[pl.BlockSpec(memory_space=pltpu.SMEM), hbm, hbm],
        out_specs=[pl.BlockSpec(memory_space=pltpu.VMEM)] * 2,
        scratch_shapes=[
            vmem((16, 64, 512), F32),
            vmem((16, 64, 512), F32),
            vmem((1024, 1024), BF16),
            vmem((1024, 1024), BF16),
            vmem((SIBS, 4, 2, 64, W), F32),
            vmem((SIBS, 4, 2, 64, W), F32),
            vmem((SIBS, 1024, W), BF16),
            vmem((SIBS, 1024, W), BF16),
            vmem((4, 64, SIBS * W), F32),
            vmem((SIBS, W, W), BF16),
            vmem((SIBS, W, W), BF16),
            vmem((SIBS, 4, 16, W), F32),
            vmem((SIBS, 4, 4, 64, W), F32),
            vmem((SIBS, 6, 2, 64, W), F32),
            vmem((SIBS, 4, 64, W), F32),
            vmem((SIBS, 3, 64, W), F32),
            vmem((SIBS, 2, 16, 8, W), F32),
            vmem((SIBS, 16, 8, W), F32),
            vmem((SIBS, 16, 8, W), F32),
            vmem((SIBS, 16, 8, W), F32),
            vmem((SIBS, 8, 8, W), F32),
            vmem((SIBS, 2, 16, 8, W), F32),
            dma((2,)),
        ]
        + [dma(shape) for shape in pairs for _ in range(2)],
        compiler_params=pltpu.CompilerParams(
            collective_id=0, has_side_effects=True, vmem_limit_bytes=52 * 1024 * 1024
        ),
    )(fill_list, factor_rows, ancestor_inv.reshape(16, 2, 64, 512))
    return block, diagonal_inv + update


def solution(mesh):
    placed = (P("row", "col"), P(("row", "col"), None), P(), P())
    return jax.shard_map(
        local, mesh=mesh, in_specs=placed, out_specs=(P(("row", "col"), None), P()), check_vma=False
    )
```
